256 devices in a mesh: seq: 64 (over z, y, core), ch: 4 (over x).
Axes of the slice: x: 4, y: 4, z: 8, core: 2. Of those that a mesh axis runs over, the one named last changes fastest.
Arguments:
- signal: bfloat16 [32768, 1024], P('seq', 'ch'), may hold values from -6 to 6
- gate_values: bfloat16 [32768, 1024], P('seq', 'ch'), may hold values from -6 to 6
- cotangent: bfloat16 [32768, 1024], P('seq', 'ch'), may hold values from -6 to 6
- skip_gain: float32 [1024], P('ch'), may hold values from -3 to 3
- log_rate: float32 [1024], P('ch'), as said below
- embed_weight: float32 [33, 64], replicated, may hold values from -1 to 1
- sine_freq: float32 [64], replicated, may hold values from 1 to 8
- mid_weight: float32 [64, 64], replicated, may hold values from -0.75 to 0.75
- out_weight: float32 [64, 1024], P(None, 'ch'), may hold values from -0.75 to 0.75
Outputs:
- output: bfloat16 [32768, 1024], P('seq', 'ch')
- signal_grad: bfloat16 [32768, 1024], P('seq', 'ch')
- gate_grad: bfloat16 [32768, 1024], P('seq', 'ch')
- skip_grad: float32 [1024], P('ch')
- rate_grad: float32 [1024], P('ch')
- out_weight_grad: float32 [64, 1024], P(None, 'ch')
- embed_grad: float32 [33, 64], replicated
- mid_grad: float32 [64, 64], replicated
- freq_grad: float32 [64], replicated
The draws below stay inside these ranges and needn't reach their ends.
Inputs may be any that keep to these rules, and one draw needn't show every extreme that they name: exp(log_rate) lies between 0.25 / 32768 and 1 / 30.
All inputs are finite; a program needn't handle non-finite values.
Results may differ from the reference program's by a relative error of at most 0.0051.
Values may be sent and summed in bfloat16 or wider, within the bound.
A program may use at most 128 MiB of HBM per device.

```python
import math
import jax
import jax.numpy as jnp
from jax import lax

D = 1024
ORDER = 64
BANDS = 16
EMB = 33
LOC = 512
SEQ = 32768


def draw_log_rate(key, part):
    flag_key, slow_key, fast_key = jax.random.split(key, 3)
    keep_share = 0.5
    slow_flag = jax.random.uniform(flag_key, (D,), jnp.float32) < keep_share
    slow_log = jax.random.uniform(slow_key, (D,), jnp.float32, math.log(0.25 / SEQ), math.log(2.0 / SEQ))
    fast_log = jax.random.uniform(fast_key, (D,), jnp.float32, math.log(1.0 / max(LOC, 60)), math.log(1.0 / 30.0))
    return jnp.where(slow_flag, slow_log, fast_log).astype(jnp.float32)


def level_of(stream_key, extent, shards, least, top_value):
    loudness = 1.0
    for dim, blocks in shards:
        draws = jax.random.uniform(jax.random.fold_in(jax.random.fold_in(stream_key, 6), dim), (blocks,), jnp.float32, least / len(shards), top_value / len(shards))
        loudness = loudness * jnp.repeat(jnp.exp(draws), extent[dim] // blocks).reshape((-1,) + (1,) * (len(extent) - 1 - dim))
    return loudness


def centred(own_key, shape, spread, limit, pieces=(), kind=jnp.bfloat16):
    values = spread * jax.random.normal(own_key, shape, jnp.float32)
    if pieces:
        values = values * level_of(own_key, shape, pieces, -0.22, 0.18)
    return jnp.clip(values, -limit, limit).astype(kind)


def setup_inputs(seed: int = 0) -> dict:
    key_of = jax.random.split(jax.random.key(seed), 10)
    return {
        "signal": centred(key_of[0], (SEQ, D), 1.0, 6.0, ((0, 64), (1, 4))),
        "gate_values": centred(key_of[1], (SEQ, D), 1.0, 6.0, ((0, 64), (1, 4))),
        "cotangent": centred(key_of[2], (SEQ, D), 1.0, 6.0, ((0, 64), (1, 4))),
        "skip_gain": centred(key_of[3], (D,), 1.0, 3.0, ((0, 4),), jnp.float32),
        "log_rate": draw_log_rate(jax.random.fold_in(key_of[9], 71), 0),
        "embed_weight": centred(key_of[5], (EMB, ORDER), EMB ** -0.5, 1.0, (), jnp.float32),
        "sine_freq": jnp.clip(jnp.exp(jax.random.uniform(key_of[6], (ORDER,), jnp.float32, math.log(1.0), math.log(8.0))), 1.0, 8.0),
        "mid_weight": centred(key_of[7], (ORDER, ORDER), ORDER ** -0.5, 0.75, (), jnp.float32),
        "out_weight": centred(key_of[8], (ORDER, D), ORDER ** -0.5, 0.75, ((1, 4),), jnp.float32),
    }


highest = lax.Precision.HIGHEST
phase_modulus = 4093
band_stride = 255

def unit_angle(product, modulus):
    return (product % modulus).astype(jnp.float32) * (2.0 * math.pi / modulus)

def position_features(positions, seq_total, band_count):
    band_steps = 1 + band_stride * jnp.arange(band_count, dtype=jnp.int32)
    angles = unit_angle(positions[:, None] * band_steps[None, :], phase_modulus)
    position_ramp = positions.astype(jnp.float32)[:, None] / seq_total
    return jnp.concatenate([position_ramp, jnp.cos(angles), jnp.sin(angles)], axis=1)

def lower_layers(features, embed_weight, sine_freq, mid_weight):
    first_pre = jnp.dot(features, embed_weight, precision=highest, preferred_element_type=jnp.float32)
    first_act = jnp.sin(sine_freq[None, :] * first_pre)
    second_pre = jnp.dot(first_act, mid_weight, precision=highest, preferred_element_type=jnp.float32)
    return jnp.sin(sine_freq[None, :] * second_pre)

def make_filter(embed_weight, sine_freq, mid_weight, out_weight, log_rate):
    positions = jnp.arange(SEQ, dtype=jnp.int32)
    features = position_features(positions, SEQ, BANDS)
    upper_act = lower_layers(features, embed_weight, sine_freq, mid_weight)
    raw_filter = jnp.dot(upper_act, out_weight, precision=highest, preferred_element_type=jnp.float32)
    decay_rate = jnp.exp(log_rate)
    place = positions.astype(jnp.float32)[:, None]
    envelope = jnp.exp(-decay_rate[None, :] * place) * jnp.sqrt(2.0 * decay_rate)[None, :]
    return raw_filter * envelope

def fft_pair(first_field, second_field, conjugate):
    block_size = math.gcd(D, 128)
    block_count = D // block_size
    first_blocks = first_field.reshape(SEQ, block_count, block_size).transpose(1, 0, 2)
    second_blocks = second_field.reshape(SEQ, block_count, block_size).transpose(1, 0, 2)
    stacked = jnp.stack([first_blocks, second_blocks], axis=1)

    def one_block(field_pair):
        spectra = jnp.fft.rfft(field_pair, n=2 * SEQ, axis=1)
        left_spec = spectra[0]
        if conjugate:
            left_spec = jnp.conj(left_spec)
        return jnp.fft.irfft(left_spec * spectra[1], n=2 * SEQ, axis=0)[:SEQ]
    result = lax.map(one_block, stacked)
    return result.transpose(1, 0, 2).reshape(SEQ, D)

def reference(signal, gate_values, cotangent, skip_gain, log_rate, embed_weight, sine_freq, mid_weight, out_weight):
    signal_f = signal.astype(jnp.float32)
    gate_f = gate_values.astype(jnp.float32)
    cot_f = cotangent.astype(jnp.float32)
    kernel, filter_pull = jax.vjp(make_filter, embed_weight, sine_freq, mid_weight, out_weight, log_rate)
    conv_out = fft_pair(kernel, signal_f, False)
    mixed_sum = conv_out + skip_gain[None, :] * signal_f
    output = (gate_f * mixed_sum).astype(jnp.bfloat16)
    gate_grad = (cot_f * mixed_sum).astype(jnp.bfloat16)
    upstream_bf = (cot_f * gate_f).astype(jnp.bfloat16)
    upstream = lax.optimization_barrier(upstream_bf).astype(jnp.float32)
    signal_corr = fft_pair(kernel, upstream, True)
    kernel_grad = fft_pair(signal_f, upstream, True)
    signal_grad = (skip_gain[None, :] * upstream + signal_corr).astype(jnp.bfloat16)
    grad_scale = 1.0 / math.sqrt(SEQ)
    skip_grad = lax.optimization_barrier(jnp.sum(upstream * signal_f, axis=0)) * grad_scale
    embed_grad, freq_grad, mid_grad, out_weight_grad, rate_grad = filter_pull(kernel_grad)
    return (output, signal_grad, gate_grad, skip_grad, rate_grad * grad_scale, out_weight_grad * grad_scale, embed_grad * grad_scale, mid_grad * grad_scale, freq_grad * grad_scale)
```

```python
import math
from functools import partial

import jax
import jax.numpy as jnp
import ml_dtypes
import numpy as np
from jax import lax
from jax.experimental import pallas as pl
from jax.experimental.pallas import tpu as pltpu
from jax.sharding import PartitionSpec as P

MESH = pl.DeviceIdType.MESH
HIGH = lax.Precision.HIGHEST
F32 = jnp.float32
BF16 = jnp.bfloat16

SHARDS = 64
LOC = 512
CH = 256
SEQ = SHARDS * LOC
GROUP = CH // SHARDS
QUARTERS = LOC // 128
CHUNK = GROUP * QUARTERS
ROWS = SHARDS * CHUNK
LEAD, TAIL = 256, 128
ORDER, BANDS = 64, 16
MODULUS, STRIDE = 4093, 255
OWNERS = 32
SCALE = 1.0 / math.sqrt(SEQ)

VM = pl.BlockSpec(memory_space=pltpu.VMEM)


def split_bf16(table):
    high = table.astype(np.float32).astype(ml_dtypes.bfloat16)
    low = (table - high.astype(np.float64)).astype(np.float32).astype(ml_dtypes.bfloat16)
    return np.stack([high, low])


def transform_tables():
    lead = np.arange(LEAD)
    tail = np.arange(TAIL)
    ang1 = 2 * np.pi * ((4 * lead[:, None] + 1) * lead[None, :] % (4 * LEAD)) / (4 * LEAD)
    first = np.concatenate([np.cos(ang1), -np.sin(ang1)], axis=0)
    last = np.concatenate([np.cos(ang1).T, -np.sin(ang1).T], axis=1)
    ang2 = 2 * np.pi * (tail[:, None] * tail[None, :] % TAIL) / TAIL
    cos2, sin2 = np.cos(ang2), np.sin(ang2)
    fwd2 = np.block([[cos2, -sin2], [sin2, cos2]])
    inv2 = np.block([[cos2, sin2], [-sin2, cos2]])
    angt = 2 * np.pi * ((4 * lead[:, None] + 1) * tail[None, :]) / (4 * SEQ)
    turn = np.stack([np.cos(angt), np.sin(angt)]).astype(np.float32)
    return tuple(split_bf16(t) for t in (first, last, fwd2, inv2)) + (turn,)


def dot_t(left, right, dims, precision=HIGH):
    return lax.dot_general(
        left, right, (dims, ((), ())), precision=precision, preferred_element_type=F32
    )


def column(row):
    size = row.shape[1]
    r = lax.broadcasted_iota(jnp.int32, (size, size), 0)
    c = lax.broadcasted_iota(jnp.int32, (size, size), 1)
    return jnp.sum(jnp.where(r == c, row, 0.0), axis=1, keepdims=True)


def spread(blocks, wide, out):
    for q in range(QUARTERS):
        block = blocks(q)
        for j in range(GROUP):
            wide[pl.ds(GROUP * q + j, SHARDS, stride=CHUNK), :] = block[
                SHARDS * j : SHARDS * (j + 1)
            ]
    out[...] = wide[...].astype(BF16)


def gather_quarter(wide, q):
    return jnp.concatenate(
        [wide[pl.ds(GROUP * q + j, SHARDS, stride=CHUNK), :] for j in range(GROUP)], axis=0
    )


def pre_kernel(
    sig_ref, gate_ref, cot_ref, logr_ref, emb_ref, freq_ref, mid_ref, outw_ref,
    sig_send, up_send, ker_send, env_ref, raw_ref, feat_ref, h1_ref, a1_ref, h2_ref, a2_ref, skip_ref,
    wide, emb_pad,
):
    seq_index = lax.axis_index("seq")
    sig = sig_ref[...].astype(F32)
    up = (cot_ref[...].astype(F32) * gate_ref[...].astype(F32)).astype(BF16).astype(F32)
    skip_ref[...] = jnp.sum(sig * up, axis=0, keepdims=True)
    spread(lambda q: jnp.transpose(sig[128 * q : 128 * (q + 1)]), wide, sig_send)
    spread(lambda q: jnp.transpose(up[128 * q : 128 * (q + 1)]), wide, up_send)

    base = seq_index * LOC
    pos = base + lax.broadcasted_iota(jnp.int32, (1, LOC), 1)
    band = 1 + STRIDE * lax.broadcasted_iota(jnp.int32, (BANDS, LOC), 0)
    prod = (base + lax.broadcasted_iota(jnp.int32, (BANDS, LOC), 1)) * band
    quot = (prod.astype(F32) * (1.0 / MODULUS)).astype(jnp.int32)
    rem = prod - quot * MODULUS
    rem = jnp.where(rem < 0, rem + MODULUS, rem)
    rem = jnp.where(rem >= MODULUS, rem - MODULUS, rem)
    angle = rem.astype(F32) * (2.0 * math.pi / MODULUS)
    place = pos.astype(F32)
    feat_ref[...] = jnp.zeros_like(feat_ref)
    feat_ref[0:1, :] = place / SEQ
    feat_ref[1 : 1 + BANDS, :] = jnp.cos(angle)
    feat_ref[1 + BANDS : 1 + 2 * BANDS, :] = jnp.sin(angle)
    emb_pad[...] = jnp.zeros_like(emb_pad)
    emb_pad[0 : 1 + 2 * BANDS, :] = emb_ref[...]
    freq = column(freq_ref[...])
    h1 = dot_t(emb_pad[...], feat_ref[...], ((0,), (0,)))
    a1 = jnp.sin(freq * h1)
    h2 = dot_t(mid_ref[...], a1, ((0,), (0,)))
    a2 = jnp.sin(freq * h2)
    h1_ref[...], a1_ref[...], h2_ref[...], a2_ref[...] = h1, a1, h2, a2
    raw = dot_t(outw_ref[...], a2, ((0,), (0,)))
    raw_ref[...] = raw
    rate = jnp.exp(column(logr_ref[...]))
    env = jnp.exp(-rate * place) * jnp.sqrt(2.0 * rate)
    env_ref[...] = env
    kern = raw * env
    spread(lambda q: kern[:, 128 * q : 128 * (q + 1)], wide, ker_send)


def fft_kernel(
    sig_ref, up_ref, ker_ref, first_ref, last_ref, fwd2_ref, inv2_ref, turn_ref,
    kg_send, conv_send, corr_send,
    wide, mid_buf, spec_s, spec_u, spec_k,
):
    def dot2(left_pair, right):
        return jnp.dot(left_pair[0], right, preferred_element_type=F32) + jnp.dot(
            left_pair[1], right, preferred_element_type=F32
        )

    def forward(src, spec):
        wide[...] = src[...].astype(F32)
        seqs = jnp.concatenate(
            [wide[pl.ds(j, LEAD, stride=GROUP), :].astype(BF16) for j in range(GROUP)], axis=1
        )
        cos, sin = turn_ref[0], turn_ref[1]
        step = dot2((first_ref[0], first_ref[1]), seqs)
        for j in range(GROUP):
            re = step[:LEAD, TAIL * j : TAIL * (j + 1)]
            im = step[LEAD:, TAIL * j : TAIL * (j + 1)]
            mid_buf[LEAD * j : LEAD * (j + 1), :TAIL] = (re * cos + im * sin).astype(BF16)
            mid_buf[LEAD * j : LEAD * (j + 1), TAIL:] = (im * cos - re * sin).astype(BF16)
        turned = mid_buf[...]
        spec[...] = jnp.dot(turned, fwd2_ref[0], preferred_element_type=F32) + jnp.dot(
            turned, fwd2_ref[1], preferred_element_type=F32
        )

    def inverse(left, right, conj_left, out):
        lr, li = left[:, :TAIL], left[:, TAIL:]
        rr, ri = right[:, :TAIL], right[:, TAIL:]
        if conj_left:
            re, im = lr * rr + li * ri, lr * ri - li * rr
        else:
            re, im = lr * rr - li * ri, lr * ri + li * rr
        mid_buf[:, :TAIL] = re.astype(BF16)
        mid_buf[:, TAIL:] = im.astype(BF16)
        spec = mid_buf[...]
        step = jnp.dot(spec, inv2_ref[0], preferred_element_type=F32) + jnp.dot(
            spec, inv2_ref[1], preferred_element_type=F32
        )
        cos, sin = turn_ref[0], turn_ref[1]
        reals, imags = [], []
        for j in range(GROUP):
            re = step[LEAD * j : LEAD * (j + 1), :TAIL]
            im = step[LEAD * j : LEAD * (j + 1), TAIL:]
            reals.append((re * cos - im * sin).astype(BF16))
            imags.append((im * cos + re * sin).astype(BF16))
        both = jnp.concatenate(
            [jnp.concatenate(reals, axis=1), jnp.concatenate(imags, axis=1)], axis=0
        )
        field = dot2((last_ref[0], last_ref[1]), both) * (1.0 / SEQ)
        for j in range(GROUP):
            wide[pl.ds(j, LEAD, stride=GROUP), :] = field[:, TAIL * j : TAIL * (j + 1)]
        out[...] = wide[...].astype(BF16)

    forward(sig_ref, spec_s)
    forward(up_ref, spec_u)
    inverse(spec_s, spec_u, True, kg_send)
    forward(ker_ref, spec_k)
    inverse(spec_k, spec_s, False, conv_send)
    inverse(spec_k, spec_u, True, corr_send)


def post_kernel(
    kg_ref, conv_ref, corr_ref, sig_ref, gate_ref, cot_ref, gain_ref, logr_ref, freq_ref, mid_ref, outw_ref,
    env_ref, raw_ref, feat_ref, h1_ref, a1_ref, h2_ref, a2_ref, skip_ref,
    out_ref, sgrad_ref, ggrad_ref, pack_ref,
    wide,
):
    place = (lax.axis_index("seq") * LOC + lax.broadcasted_iota(jnp.int32, (1, LOC), 1)).astype(F32)
    wide[...] = kg_ref[...].astype(F32)
    kgrad = jnp.concatenate([gather_quarter(wide, q) for q in range(QUARTERS)], axis=1)
    scaled = kgrad * env_ref[...]
    rate = jnp.exp(column(logr_ref[...]))
    weighted = scaled * raw_ref[...] * (0.5 - rate * place)
    ones = jnp.ones((8, LOC), F32)
    rate_part = dot_t(ones, weighted, ((1,), (1,)))[0:1]
    a2 = a2_ref[...]
    out_part = dot_t(a2, scaled, ((1,), (1,)))
    g2 = jnp.dot(outw_ref[...], scaled, precision=HIGH, preferred_element_type=F32)
    freq = column(freq_ref[...])
    h1, h2, a1 = h1_ref[...], h2_ref[...], a1_ref[...]
    c2 = jnp.cos(freq * h2) * g2
    d2 = freq * c2
    mid_part = dot_t(a1, d2, ((1,), (1,)))
    g1 = jnp.dot(mid_ref[...], d2, precision=HIGH, preferred_element_type=F32)
    c1 = jnp.cos(freq * h1) * g1
    d1 = freq * c1
    emb_part = dot_t(feat_ref[...], d1, ((1,), (1,)))
    freq_part = dot_t(ones, c2 * h2 + c1 * h1, ((1,), (1,)))[0:1]

    pack_ref[...] = jnp.zeros_like(pack_ref)
    pack_ref[pl.ds(0, 64, stride=4), :] = out_part[:, :128]
    pack_ref[pl.ds(1, 64, stride=4), :] = out_part[:, 128:]
    emb_cols = jnp.concatenate(
        [emb_part, jnp.broadcast_to(freq_part, (8, ORDER)), jnp.zeros((16, ORDER), F32)], axis=0
    )
    pack_ref[pl.ds(2, 64, stride=4), :] = jnp.concatenate([mid_part, emb_cols], axis=1)
    skip = skip_ref[...]
    pack_ref[3:4, :] = skip[:, :128]
    pack_ref[7:8, :] = skip[:, 128:]
    pack_ref[11:12, :] = rate_part[:, :128]
    pack_ref[15:16, :] = rate_part[:, 128:]

    gain = gain_ref[...]
    wide[...] = conv_ref[...].astype(F32)
    for q in range(QUARTERS):
        rows = slice(128 * q, 128 * (q + 1))
        conv = jnp.transpose(gather_quarter(wide, q))
        mixed = conv + gain * sig_ref[rows].astype(F32)
        gate = gate_ref[rows].astype(F32)
        cot = cot_ref[rows].astype(F32)
        out_ref[rows] = (gate * mixed).astype(BF16)
        ggrad_ref[rows] = (cot * mixed).astype(BF16)
    wide[...] = corr_ref[...].astype(F32)
    for q in range(QUARTERS):
        rows = slice(128 * q, 128 * (q + 1))
        corr = jnp.transpose(gather_quarter(wide, q))
        up = (cot_ref[rows].astype(F32) * gate_ref[rows].astype(F32)).astype(BF16).astype(F32)
        sgrad_ref[rows] = (gain * up + corr).astype(BF16)


def meet_seq(me, extra=()):
    barrier = pltpu.get_barrier_semaphore()

    def greet(i, carry):
        pl.semaphore_signal(
            barrier, inc=1, device_id={"seq": lax.rem(me + i, SHARDS)}, device_id_type=MESH
        )
        return carry

    lax.fori_loop(1, SHARDS, greet, 0)
    for peer in extra:
        pl.semaphore_signal(barrier, inc=1, device_id={"ch": peer}, device_id_type=MESH)
    pl.semaphore_wait(barrier, SHARDS - 1 + len(extra))


def exchange_kernel(count, *refs):
    sends, recvs = refs[:count], refs[count : 2 * count]
    send_sem, recv_sem, own_sem = refs[2 * count :]
    me = lax.axis_index("seq")
    meet_seq(me)
    mine = pl.ds(pl.multiple_of(me * CHUNK, CHUNK), CHUNK)

    for f in range(count):
        def push(i, carry, f=f):
            peer = lax.rem(me + i, SHARDS)
            theirs = pl.ds(pl.multiple_of(peer * CHUNK, CHUNK), CHUNK)
            pltpu.make_async_remote_copy(
                src_ref=sends[f].at[theirs],
                dst_ref=recvs[f].at[mine],
                send_sem=send_sem.at[f],
                recv_sem=recv_sem.at[f],
                device_id={"seq": peer},
                device_id_type=MESH,
            ).start()
            return carry

        lax.fori_loop(1, SHARDS, push, 0)
        pltpu.make_async_copy(sends[f].at[mine], recvs[f].at[mine], own_sem.at[f]).start()
    for f in range(count):
        rest = pl.ds(0, ROWS - CHUNK)
        done = pltpu.make_async_remote_copy(
            src_ref=sends[f].at[rest],
            dst_ref=recvs[f].at[rest],
            send_sem=send_sem.at[f],
            recv_sem=recv_sem.at[f],
            device_id={"seq": me},
            device_id_type=MESH,
        )
        done.wait_send()
        done.wait_recv()
        pltpu.make_async_copy(sends[f].at[mine], recvs[f].at[mine], own_sem.at[f]).wait()


def exchange(fields, collective_id):
    count = len(fields)
    return pl.pallas_call(
        partial(exchange_kernel, count),
        out_shape=[jax.ShapeDtypeStruct((ROWS, 128), BF16)] * count,
        in_specs=[VM] * count,
        out_specs=[VM] * count,
        scratch_shapes=[pltpu.SemaphoreType.DMA((count,))] * 3,
        compiler_params=pltpu.CompilerParams(collective_id=collective_id, has_side_effects=True),
        name="exchange%d" % collective_id,
    )(*fields)


def reduce_kernel(
    pack_ref, out_ref, skip_ref, rate_ref, emb_ref, mid_ref, freq_ref,
    parts, mine_buf, cross, total, sems,
):
    me = lax.axis_index("seq")
    lane = lax.axis_index("ch")
    others = [lax.rem(lane + i, 4) for i in (1, 2, 3)]
    meet_seq(me, others)
    owner = lax.div(me, 2)
    own_rows = pl.ds(pl.multiple_of(owner * 8, 8), 8)
    is_owner = lax.rem(me, 2) == 0

    def push(i, carry):
        slot = lax.rem(owner + i, OWNERS)
        pltpu.make_async_remote_copy(
            src_ref=pack_ref.at[pl.ds(pl.multiple_of(slot * 8, 8), 8)],
            dst_ref=parts.at[me],
            send_sem=sems.at[0],
            recv_sem=sems.at[1],
            device_id={"seq": 2 * slot},
            device_id_type=MESH,
        ).start()
        return carry

    lax.fori_loop(1, OWNERS, push, 0)

    @pl.when(jnp.logical_not(is_owner))
    def _():
        push(0, 0)

    def recv_rows(n, send, recv):
        return pltpu.make_async_remote_copy(
            src_ref=parts.at[pl.ds(0, n)],
            dst_ref=parts.at[pl.ds(0, n)],
            send_sem=sems.at[send],
            recv_sem=sems.at[recv],
            device_id={"seq": me},
            device_id_type=MESH,
        )

    @pl.when(is_owner)
    def _():
        recv_rows(SHARDS - 1, 0, 1).wait_recv()
        parts[me] = pack_ref[own_rows]
        acc = parts[0]
        for s in range(1, SHARDS):
            acc = acc + parts[s]
        mine_buf[...] = acc
        for n, other in enumerate(others):
            pltpu.make_async_remote_copy(
                src_ref=mine_buf,
                dst_ref=cross.at[2 - n],
                send_sem=sems.at[2],
                recv_sem=sems.at[3],
                device_id={"ch": other},
                device_id_type=MESH,
            ).start()
        recv_rows(3, 2, 3).wait_recv()
        shared = lax.rem(lax.broadcasted_iota(jnp.int32, (8, 128), 0), 4) == 2
        acc = acc + jnp.where(shared, cross[0] + cross[1] + cross[2], 0.0)
        total[own_rows] = acc
        recv_rows(3, 2, 3).wait_send()

        def tell(i, carry):
            pltpu.make_async_remote_copy(
                src_ref=total.at[own_rows],
                dst_ref=total.at[own_rows],
                send_sem=sems.at[4],
                recv_sem=sems.at[5],
                device_id={"seq": lax.rem(me + i, SHARDS)},
                device_id_type=MESH,
            ).start()
            return carry

        lax.fori_loop(1, SHARDS, tell, 0)
        recv_rows(OWNERS - 1, 4, 5).wait_recv()
        recv_rows(SHARDS - 1, 4, 5).wait_send()
        recv_rows(OWNERS - 1, 0, 1).wait_send()

    @pl.when(jnp.logical_not(is_owner))
    def _():
        recv_rows(OWNERS, 0, 1).wait_send()
        recv_rows(OWNERS, 4, 5).wait_recv()

    out_ref[:, :128] = total[pl.ds(0, 64, stride=4), :] * SCALE
    out_ref[:, 128:] = total[pl.ds(1, 64, stride=4), :] * SCALE
    shared_rows = total[pl.ds(2, 64, stride=4), :] * SCALE
    mid_ref[...] = shared_rows[:, :ORDER]
    emb_ref[...] = shared_rows[: 1 + 2 * BANDS, ORDER:]
    freq_ref[...] = shared_rows[40:41, ORDER:]
    skip_ref[:, :128] = total[3:4, :] * SCALE
    skip_ref[:, 128:] = total[7:8, :] * SCALE
    rate_ref[:, :128] = total[11:12, :] * SCALE
    rate_ref[:, 128:] = total[15:16, :] * SCALE


def reduce_params(pack):
    shapes = [(ORDER, CH), (1, CH), (1, CH), (1 + 2 * BANDS, ORDER), (ORDER, ORDER), (1, ORDER)]
    return pl.pallas_call(
        reduce_kernel,
        out_shape=[jax.ShapeDtypeStruct(s, F32) for s in shapes],
        in_specs=[VM],
        out_specs=[VM] * len(shapes),
        scratch_shapes=[
            pltpu.VMEM((SHARDS, 8, 128), F32),
            pltpu.VMEM((8, 128), F32),
            pltpu.VMEM((3, 8, 128), F32),
            pltpu.VMEM((256, 128), F32),
            pltpu.SemaphoreType.DMA((6,)),
        ],
        compiler_params=pltpu.CompilerParams(collective_id=3, has_side_effects=True),
        name="reduce_params",
    )(pack)


def on_device(signal, gate_values, cotangent, skip_gain, log_rate, embed_weight, sine_freq, mid_weight, out_weight):
    field = jax.ShapeDtypeStruct((ROWS, 128), BF16)
    full = jax.ShapeDtypeStruct((CH, LOC), F32)
    hidden = jax.ShapeDtypeStruct((ORDER, LOC), F32)
    gain, logr, freq = skip_gain[None, :], log_rate[None, :], sine_freq[None, :]
    pre = pl.pallas_call(
        pre_kernel,
        out_shape=[field] * 3
        + [full] * 2
        + [jax.ShapeDtypeStruct((40, LOC), F32)]
        + [hidden] * 4
        + [jax.ShapeDtypeStruct((1, CH), F32)],
        in_specs=[VM] * 8,
        out_specs=[VM] * 11,
        scratch_shapes=[pltpu.VMEM((ROWS, 128), F32), pltpu.VMEM((40, ORDER), F32)],
        name="pre",
    )(signal, gate_values, cotangent, logr, embed_weight, freq, mid_weight, out_weight)
    sends, kept = pre[:3], pre[3:]
    recvs = exchange(sends, 1)
    tables = transform_tables()
    fields = pl.pallas_call(
        fft_kernel,
        out_shape=[field] * 3,
        in_specs=[VM] * 8,
        out_specs=[VM] * 3,
        scratch_shapes=[pltpu.VMEM((ROWS, 128), F32), pltpu.VMEM((ROWS, 256), BF16)]
        + [pltpu.VMEM((ROWS, 256), F32)] * 3,
        name="transform",
    )(*recvs, *tables)
    back = exchange(fields, 2)
    wide_out = jax.ShapeDtypeStruct((LOC, CH), BF16)
    output, signal_grad, gate_grad, pack = pl.pallas_call(
        post_kernel,
        out_shape=[wide_out] * 3 + [jax.ShapeDtypeStruct((256, 128), F32)],
        in_specs=[VM] * 19,
        out_specs=[VM] * 4,
        scratch_shapes=[pltpu.VMEM((ROWS, 128), F32)],
        name="post",
    )(*back, signal, gate_values, cotangent, gain, logr, freq, mid_weight, out_weight, *kept)
    out_sum, skip_sum, rate_sum, emb_sum, mid_sum, freq_sum = reduce_params(pack)
    return (
        output, signal_grad, gate_grad, skip_sum[0], rate_sum[0], out_sum, emb_sum, mid_sum, freq_sum[0],
    )


def solution(mesh):
    wide, flat, rep = P("seq", "ch"), P("ch"), P()
    return jax.shard_map(
        on_device,
        mesh=mesh,
        in_specs=(wide, wide, wide, flat, flat, rep, rep, rep, P(None, "ch")),
        out_specs=(wide, wide, wide, flat, flat, P(None, "ch"), rep, rep, rep),
        check_vma=False,
    )
```

```python
import math
from functools import partial

import jax
import jax.numpy as jnp
import ml_dtypes
import numpy as np
from jax import lax
from jax.experimental import pallas as pl
from jax.experimental.pallas import tpu as pltpu
from jax.sharding import PartitionSpec as P

MESH = pl.DeviceIdType.MESH
HIGH = lax.Precision.HIGHEST
F32 = jnp.float32
BF16 = jnp.bfloat16

SHARDS = 64
LOC = 512
CH = 256
SEQ = SHARDS * LOC
GROUP = CH // SHARDS
QUARTERS = LOC // 128
CHUNK = GROUP * QUARTERS
ROWS = SHARDS * CHUNK
LEAD, TAIL = 256, 128
ORDER, BANDS = 64, 16
MODULUS, STRIDE = 4093, 255
OWNERS = 16
PART = 16
SCALE = 1.0 / math.sqrt(SEQ)

VM = pl.BlockSpec(memory_space=pltpu.VMEM)


def split_bf16(table):
    high = table.astype(np.float32).astype(ml_dtypes.bfloat16)
    low = (table - high.astype(np.float64)).astype(np.float32).astype(ml_dtypes.bfloat16)
    return np.stack([high, low])


def transform_tables():
    lead = np.arange(LEAD)
    tail = np.arange(TAIL)
    ang1 = 2 * np.pi * ((4 * lead[:, None] + 1) * lead[None, :] % (4 * LEAD)) / (4 * LEAD)
    first = np.concatenate([np.cos(ang1), -np.sin(ang1)], axis=0)
    last = np.concatenate([np.cos(ang1).T, -np.sin(ang1).T], axis=1)
    ang2 = 2 * np.pi * (tail[:, None] * tail[None, :] % TAIL) / TAIL
    cos2, sin2 = np.cos(ang2), np.sin(ang2)
    fwd2 = np.block([[cos2, -sin2], [sin2, cos2]])
    inv2 = np.block([[cos2, sin2], [-sin2, cos2]])
    angt = 2 * np.pi * ((4 * lead[:, None] + 1) * tail[None, :]) / (4 * SEQ)
    turn = np.stack([np.cos(angt), np.sin(angt)]).astype(np.float32)
    return tuple(split_bf16(t) for t in (first, last, fwd2, inv2)) + (turn,)


def dot_t(left, right, dims, precision=HIGH):
    return lax.dot_general(
        left, right, (dims, ((), ())), precision=precision, preferred_element_type=F32
    )


def column(row):
    size = row.shape[1]
    r = lax.broadcasted_iota(jnp.int32, (size, size), 0)
    c = lax.broadcasted_iota(jnp.int32, (size, size), 1)
    return jnp.sum(jnp.where(r == c, row, 0.0), axis=1, keepdims=True)


def spread(blocks, wide, out):
    for q in range(QUARTERS):
        block = blocks(q)
        for j in range(GROUP):
            wide[pl.ds(GROUP * q + j, SHARDS, stride=CHUNK), :] = block[
                SHARDS * j : SHARDS * (j + 1)
            ]
    out[...] = wide[...].astype(BF16)


def gather_quarter(wide, q):
    return jnp.concatenate(
        [wide[pl.ds(GROUP * q + j, SHARDS, stride=CHUNK), :] for j in range(GROUP)], axis=0
    )


ANY = pl.BlockSpec(memory_space=pl.ANY)


def relative(me, dz, dy, dc):
    z, y, c = lax.div(me, 8), lax.rem(lax.div(me, 2), 4), lax.rem(me, 2)
    return (lax.rem(z + dz, 8) * 4 + lax.rem(y + dy, 4)) * 2 + lax.rem(c + dc, 2)


def far_first(me, i):
    left = 63 - i
    m = lax.rem(left, 8)
    dz = jnp.where(lax.rem(m, 2) == 1, lax.div(m + 1, 2), lax.rem(8 - lax.div(m, 2), 8))
    return relative(me, dz, lax.rem(lax.div(left, 8), 4), lax.div(left, 32))


def main_kernel(
    sig_hbm, gate_hbm, cot_hbm, gain_ref, logr_ref, emb_ref, freq_ref, mid_ref, outw_ref,
    first_hbm, last_hbm, fwd2_hbm, inv2_hbm, turn_hbm,
    out_ref, sgrad_ref, ggrad_ref, total_ref,
    sig_ref, gate_ref, cot_ref, first_ref, last_ref, fwd2_ref, inv2_ref, turn_ref,
    wide, emb_pad, env_ref, raw_ref, feat_ref, mid_buf, spec_s, spec_u, spec_k,
    sends, recvs, pack32, pack16, parts, mine_buf, cross, total16,
    load_sem, send_sem, recv_sem, own_sem, sums_sem,
):
    me = lax.axis_index("seq")
    lane = lax.axis_index("ch")
    others = [lax.rem(lane + i, 4) for i in (1, 2, 3)]
    barrier = pltpu.get_barrier_semaphore()

    def greet(i, carry):
        pl.semaphore_signal(
            barrier, inc=1, device_id={"seq": lax.rem(me + i, SHARDS)}, device_id_type=MESH
        )
        return carry

    lax.fori_loop(1, SHARDS, greet, 0)
    for peer in others:
        pl.semaphore_signal(barrier, inc=1, device_id={"ch": peer}, device_id_type=MESH)

    loads = [
        pltpu.make_async_copy(a, b, load_sem.at[n])
        for n, (a, b) in enumerate(
            (
                (sig_hbm, sig_ref), (gate_hbm, gate_ref), (cot_hbm, cot_ref), (first_hbm, first_ref),
                (turn_hbm, turn_ref), (fwd2_hbm, fwd2_ref), (inv2_hbm, inv2_ref), (last_hbm, last_ref),
            )
        )
    ]
    for load in loads:
        load.start()

    mine = pl.ds(pl.multiple_of(me * CHUNK, CHUNK), CHUNK)

    def push(f):
        def one(i, carry):
            peer = far_first(me, i)
            theirs = pl.ds(pl.multiple_of(peer * CHUNK, CHUNK), CHUNK)
            pltpu.make_async_remote_copy(
                src_ref=sends.at[f, theirs],
                dst_ref=recvs.at[f, mine],
                send_sem=send_sem.at[f],
                recv_sem=recv_sem.at[f],
                device_id={"seq": peer},
                device_id_type=MESH,
            ).start()
            return carry

        lax.fori_loop(0, SHARDS - 1, one, 0)
        pltpu.make_async_copy(sends.at[f, mine], recvs.at[f, mine], own_sem.at[f]).start()

    def all_of(f):
        rest = pl.ds(0, ROWS - CHUNK)
        return pltpu.make_async_remote_copy(
            src_ref=sends.at[f, rest],
            dst_ref=recvs.at[f, rest],
            send_sem=send_sem.at[f],
            recv_sem=recv_sem.at[f],
            device_id={"seq": me},
            device_id_type=MESH,
        )

    def arrive(f):
        pltpu.make_async_copy(sends.at[f, mine], recvs.at[f, mine], own_sem.at[f]).wait()
        all_of(f).wait_recv()

    loads[0].wait()
    spread(lambda q: jnp.transpose(sig_ref[128 * q : 128 * (q + 1)].astype(F32)), wide, sends.at[0])
    loads[1].wait()
    loads[2].wait()

    def upstream(rows):
        return (cot_ref[rows].astype(F32) * gate_ref[rows].astype(F32)).astype(BF16).astype(F32)

    spread(lambda q: jnp.transpose(upstream(slice(128 * q, 128 * (q + 1)))), wide, sends.at[1])
    pl.semaphore_wait(barrier, SHARDS - 1 + len(others))
    push(0)
    push(1)

    base = me * LOC
    band = 1 + STRIDE * lax.broadcasted_iota(jnp.int32, (BANDS, LOC), 0)
    prod = (base + lax.broadcasted_iota(jnp.int32, (BANDS, LOC), 1)) * band
    quot = (prod.astype(F32) * (1.0 / MODULUS)).astype(jnp.int32)
    rem = prod - quot * MODULUS
    rem = jnp.where(rem < 0, rem + MODULUS, rem)
    rem = jnp.where(rem >= MODULUS, rem - MODULUS, rem)
    angle = rem.astype(F32) * (2.0 * math.pi / MODULUS)
    place = (base + lax.broadcasted_iota(jnp.int32, (1, LOC), 1)).astype(F32)
    feat_ref[...] = jnp.zeros_like(feat_ref)
    feat_ref[0:1, :] = place / SEQ
    feat_ref[1 : 1 + BANDS, :] = jnp.cos(angle)
    feat_ref[1 + BANDS : 1 + 2 * BANDS, :] = jnp.sin(angle)
    emb_pad[...] = jnp.zeros_like(emb_pad)
    emb_pad[0 : 1 + 2 * BANDS, :] = emb_ref[...]
    freq = column(freq_ref[...])
    h1 = dot_t(emb_pad[...], feat_ref[...], ((0,), (0,)))
    a1 = jnp.sin(freq * h1)
    h2 = dot_t(mid_ref[...], a1, ((0,), (0,)))
    a2 = jnp.sin(freq * h2)
    raw = dot_t(outw_ref[...], a2, ((0,), (0,)))
    rate = jnp.exp(column(logr_ref[...]))
    env = jnp.exp(-rate * place) * jnp.sqrt(2.0 * rate)
    env_ref[...] = env
    raw_ref[...] = raw * (0.5 - rate * place)
    kern = raw * env
    spread(lambda q: kern[:, 128 * q : 128 * (q + 1)], wide, sends.at[2])
    push(2)

    def dot2(left_pair, right):
        return jnp.dot(left_pair[0], right, preferred_element_type=F32) + jnp.dot(
            left_pair[1], right, preferred_element_type=F32
        )

    def forward(f, spec):
        wide[...] = recvs[f].astype(F32)
        seqs = jnp.concatenate(
            [wide[pl.ds(j, LEAD, stride=GROUP), :].astype(BF16) for j in range(GROUP)], axis=1
        )
        cos, sin = turn_ref[0], turn_ref[1]
        step = dot2((first_ref[0], first_ref[1]), seqs)
        for j in range(GROUP):
            re = step[:LEAD, TAIL * j : TAIL * (j + 1)]
            im = step[LEAD:, TAIL * j : TAIL * (j + 1)]
            mid_buf[LEAD * j : LEAD * (j + 1), :TAIL] = (re * cos + im * sin).astype(BF16)
            mid_buf[LEAD * j : LEAD * (j + 1), TAIL:] = (im * cos - re * sin).astype(BF16)
        turned = mid_buf[...]
        spec[...] = jnp.dot(turned, fwd2_ref[0], preferred_element_type=F32) + jnp.dot(
            turned, fwd2_ref[1], preferred_element_type=F32
        )

    def inverse(left, right, conj_left, f):
        lr, li = left[:, :TAIL], left[:, TAIL:]
        rr, ri = right[:, :TAIL], right[:, TAIL:]
        if conj_left:
            re, im = lr * rr + li * ri, lr * ri - li * rr
        else:
            re, im = lr * rr - li * ri, lr * ri + li * rr
        mid_buf[:, :TAIL] = re.astype(BF16)
        mid_buf[:, TAIL:] = im.astype(BF16)
        spec = mid_buf[...]
        step = jnp.dot(spec, inv2_ref[0], preferred_element_type=F32) + jnp.dot(
            spec, inv2_ref[1], preferred_element_type=F32
        )
        cos, sin = turn_ref[0], turn_ref[1]
        reals, imags = [], []
        for j in range(GROUP):
            re = step[LEAD * j : LEAD * (j + 1), :TAIL]
            im = step[LEAD * j : LEAD * (j + 1), TAIL:]
            reals.append((re * cos - im * sin).astype(BF16))
            imags.append((im * cos + re * sin).astype(BF16))
        both = jnp.concatenate(
            [jnp.concatenate(reals, axis=1), jnp.concatenate(imags, axis=1)], axis=0
        )
        field = dot2((last_ref[0], last_ref[1]), both) * (1.0 / SEQ)
        for j in range(GROUP):
            wide[pl.ds(j, LEAD, stride=GROUP), :] = field[:, TAIL * j : TAIL * (j + 1)]
        sends[f] = wide[...].astype(BF16)

    for load in loads[3:]:
        load.wait()
    arrive(0)
    forward(0, spec_s)
    arrive(1)
    forward(1, spec_u)
    inverse(spec_s, spec_u, True, 3)
    push(3)
    arrive(2)
    forward(2, spec_k)
    inverse(spec_k, spec_s, False, 4)
    push(4)
    inverse(spec_k, spec_u, True, 5)

    skip = jnp.zeros((1, CH), F32)
    for q in range(QUARTERS):
        rows = slice(128 * q, 128 * (q + 1))
        skip = skip + jnp.sum(sig_ref[rows].astype(F32) * upstream(rows), axis=0, keepdims=True)
    cos1, cos2 = jnp.cos(freq * h1), jnp.cos(freq * h2)
    arrive(3)
    wide[...] = recvs[3].astype(F32)
    kgrad = jnp.concatenate([gather_quarter(wide, q) for q in range(QUARTERS)], axis=1)
    scaled = kgrad * env_ref[...]
    ones = jnp.ones((8, LOC), F32)
    rate_part = dot_t(ones, scaled * raw_ref[...], ((1,), (1,)))[0:1]
    out_part = dot_t(a2, scaled, ((1,), (1,)))
    g2 = jnp.dot(outw_ref[...], scaled, precision=HIGH, preferred_element_type=F32)
    c2 = cos2 * g2
    d2 = freq * c2
    mid_part = dot_t(a1, d2, ((1,), (1,)))
    c1 = cos1 * jnp.dot(mid_ref[...], d2, precision=HIGH, preferred_element_type=F32)
    emb_part = dot_t(feat_ref[...], freq * c1, ((1,), (1,)))
    freq_part = dot_t(ones, c2 * h2 + c1 * h1, ((1,), (1,)))[0:1]

    pack32[pl.ds(0, 64, stride=4), :] = out_part[:, :128]
    pack32[pl.ds(1, 64, stride=4), :] = out_part[:, 128:]
    emb_cols = jnp.concatenate(
        [emb_part, jnp.broadcast_to(freq_part, (8, ORDER)), jnp.zeros((16, ORDER), F32)], axis=0
    )
    pack32[pl.ds(2, 64, stride=4), :] = jnp.concatenate([mid_part, emb_cols], axis=1)
    pack32[pl.ds(3, 64, stride=4), :] = jnp.zeros((64, 128), F32)
    pack32[3:4, :] = skip[:, :128]
    pack32[7:8, :] = skip[:, 128:]
    pack32[11:12, :] = rate_part[:, :128]
    pack32[15:16, :] = rate_part[:, 128:]
    pack16[...] = pack32[...].astype(BF16)

    slot_of = lax.div(me, 4)
    is_owner = lax.rem(me, 4) == 0
    own_rows = pl.ds(pl.multiple_of(slot_of * PART, PART), PART)

    def hand_in(i, carry):
        slot = lax.rem(slot_of + i, OWNERS)
        pltpu.make_async_remote_copy(
            src_ref=pack16.at[pl.ds(pl.multiple_of(slot * PART, PART), PART)],
            dst_ref=parts.at[me],
            send_sem=sums_sem.at[0],
            recv_sem=sums_sem.at[1],
            device_id={"seq": 4 * slot},
            device_id_type=MESH,
        ).start()
        return carry

    lax.fori_loop(1, OWNERS, hand_in, 0)

    @pl.when(jnp.logical_not(is_owner))
    def _():
        hand_in(0, 0)

    push(5)

    def sums(n, send, recv):
        return pltpu.make_async_remote_copy(
            src_ref=parts.at[pl.ds(0, n)],
            dst_ref=parts.at[pl.ds(0, n)],
            send_sem=sums_sem.at[send],
            recv_sem=sums_sem.at[recv],
            device_id={"seq": me},
            device_id_type=MESH,
        )

    gain = gain_ref[...]
    arrive(4)
    wide[...] = recvs[4].astype(F32)
    for q in range(QUARTERS):
        rows = slice(128 * q, 128 * (q + 1))
        mixed = jnp.transpose(gather_quarter(wide, q)) + gain * sig_ref[rows].astype(F32)
        out_ref[rows] = (gate_ref[rows].astype(F32) * mixed).astype(BF16)
        ggrad_ref[rows] = (cot_ref[rows].astype(F32) * mixed).astype(BF16)

    @pl.when(is_owner)
    def _():
        sums(SHARDS - 1, 0, 1).wait_recv()
        parts[me] = pack16[own_rows]
        acc = parts[0].astype(F32)
        for s in range(1, SHARDS):
            acc = acc + parts[s].astype(F32)
        mine_buf[...] = acc
        for n, other in enumerate(others):
            pltpu.make_async_remote_copy(
                src_ref=mine_buf,
                dst_ref=cross.at[2 - n],
                send_sem=sums_sem.at[2],
                recv_sem=sums_sem.at[3],
                device_id={"ch": other},
                device_id_type=MESH,
            ).start()
        three = pltpu.make_async_remote_copy(
            src_ref=cross,
            dst_ref=cross,
            send_sem=sums_sem.at[2],
            recv_sem=sums_sem.at[3],
            device_id={"seq": me},
            device_id_type=MESH,
        )
        three.wait_recv()
        shared = lax.rem(lax.broadcasted_iota(jnp.int32, (PART, 128), 0), 4) == 2
        acc = acc + jnp.where(shared, cross[0] + cross[1] + cross[2], 0.0)
        total16[own_rows] = acc.astype(BF16)

        def tell(i, carry):
            pltpu.make_async_remote_copy(
                src_ref=total16.at[own_rows],
                dst_ref=total16.at[own_rows],
                send_sem=sums_sem.at[4],
                recv_sem=sums_sem.at[5],
                device_id={"seq": far_first(me, i)},
                device_id_type=MESH,
            ).start()
            return carry

        lax.fori_loop(0, SHARDS - 1, tell, 0)
        three.wait_send()

    arrive(5)
    wide[...] = recvs[5].astype(F32)
    for q in range(QUARTERS):
        rows = slice(128 * q, 128 * (q + 1))
        corr = jnp.transpose(gather_quarter(wide, q))
        sgrad_ref[rows] = (gain * upstream(rows) + corr).astype(BF16)

    for f in range(6):
        all_of(f).wait_send()

    @pl.when(is_owner)
    def _():
        sums(OWNERS - 1, 4, 5).wait_recv()
        sums(SHARDS - 1, 4, 5).wait_send()
        sums(OWNERS - 1, 0, 1).wait_send()

    @pl.when(jnp.logical_not(is_owner))
    def _():
        sums(OWNERS, 0, 1).wait_send()
        sums(OWNERS, 4, 5).wait_recv()

    total_ref[...] = total16[...].astype(F32) * SCALE


def unpack_kernel(total, out_ref, skip_ref, rate_ref, emb_ref, mid_ref, freq_ref):
    out_ref[:, :128] = total[pl.ds(0, 64, stride=4), :]
    out_ref[:, 128:] = total[pl.ds(1, 64, stride=4), :]
    shared_rows = total[pl.ds(2, 64, stride=4), :]
    mid_ref[...] = shared_rows[:, :ORDER]
    emb_ref[...] = shared_rows[: 1 + 2 * BANDS, ORDER:]
    freq_ref[...] = shared_rows[40:41, ORDER:]
    skip_ref[:, :128] = total[3:4, :]
    skip_ref[:, 128:] = total[7:8, :]
    rate_ref[:, :128] = total[11:12, :]
    rate_ref[:, 128:] = total[15:16, :]


def on_device(signal, gate_values, cotangent, skip_gain, log_rate, embed_weight, sine_freq, mid_weight, out_weight):
    tables = transform_tables()
    wide_out = jax.ShapeDtypeStruct((LOC, CH), BF16)
    output, signal_grad, gate_grad, total = pl.pallas_call(
        main_kernel,
        out_shape=[wide_out] * 3 + [jax.ShapeDtypeStruct((256, 128), F32)],
        in_specs=[ANY] * 3 + [VM] * 6 + [ANY] * 5,
        out_specs=[VM] * 4,
        scratch_shapes=[pltpu.VMEM((LOC, CH), BF16)] * 3
        + [pltpu.VMEM(t.shape, t.dtype) for t in tables]
        + [
            pltpu.VMEM((ROWS, 128), F32),
            pltpu.VMEM((40, ORDER), F32),
            pltpu.VMEM((CH, LOC), F32),
            pltpu.VMEM((CH, LOC), F32),
            pltpu.VMEM((40, LOC), F32),
            pltpu.VMEM((ROWS, 256), BF16),
            pltpu.VMEM((ROWS, 256), F32),
            pltpu.VMEM((ROWS, 256), F32),
            pltpu.VMEM((ROWS, 256), F32),
            pltpu.VMEM((6, ROWS, 128), BF16),
            pltpu.VMEM((6, ROWS, 128), BF16),
            pltpu.VMEM((256, 128), F32),
            pltpu.VMEM((256, 128), BF16),
            pltpu.VMEM((SHARDS, PART, 128), BF16),
            pltpu.VMEM((PART, 128), F32),
            pltpu.VMEM((3, PART, 128), F32),
            pltpu.VMEM((256, 128), BF16),
            pltpu.SemaphoreType.DMA((8,)),
            pltpu.SemaphoreType.DMA((6,)),
            pltpu.SemaphoreType.DMA((6,)),
            pltpu.SemaphoreType.DMA((6,)),
            pltpu.SemaphoreType.DMA((6,)),
        ],
        compiler_params=pltpu.CompilerParams(collective_id=1, has_side_effects=True),
        name="hyena",
    )(
        signal, gate_values, cotangent, skip_gain[None, :], log_rate[None, :], embed_weight,
        sine_freq[None, :], mid_weight, out_weight, *tables,
    )
    shapes = [(ORDER, CH), (1, CH), (1, CH), (1 + 2 * BANDS, ORDER), (ORDER, ORDER), (1, ORDER)]
    out_sum, skip_sum, rate_sum, emb_sum, mid_sum, freq_sum = pl.pallas_call(
        unpack_kernel,
        out_shape=[jax.ShapeDtypeStruct(s, F32) for s in shapes],
        in_specs=[VM],
        out_specs=[VM] * len(shapes),
        name="unpack",
    )(total)
    return (
        output, signal_grad, gate_grad, skip_sum[0], rate_sum[0], out_sum, emb_sum, mid_sum, freq_sum[0],
    )


def solution(mesh):
    wide, flat, rep = P("seq", "ch"), P("ch"), P()
    return jax.shard_map(
        on_device,
        mesh=mesh,
        in_specs=(wide, wide, wide, flat, flat, rep, rep, rep, P(None, "ch")),
        out_specs=(wide, wide, wide, flat, flat, P(None, "ch"), rep, rep, rep),
        check_vma=False,
    )
```
